32 devices in a mesh: groups: 2 (over y), expert: 4 (over z), tensor: 4 (over x, core).
Axes of the slice: x: 2, y: 2, z: 4, core: 2. Of those that a mesh axis runs over, the one named last changes fastest.
Arguments:
- tokens: bfloat16 [1024, 6144], P(('groups', 'expert', 'tensor')), parts along dimension 0, may hold values from -6 to 6
- expert_ids: int32 [1024, 2], P(('groups', 'expert', 'tensor')), parts along dimension 0, may hold values from 0 to 3, all different within a row; in each aligned block of 32 rows (0 to 31, 32 to 63, ...) at most 32 rows name the same one
- gate_scores: float32 [1024, 2], P(('groups', 'expert', 'tensor')), parts along dimension 0, may hold values from 0.1 to 1
- norm_gain: float32 [6144], replicated, may hold values from 0.1 to 1.9
- w_gate: bfloat16 [4, 6144, 1024], P('expert', None, 'tensor'), may hold values from -0.078125 to 0.078125
- w_up: bfloat16 [4, 6144, 1024], P('expert', None, 'tensor'), may hold values from -0.078125 to 0.078125
- w_down: bfloat16 [4, 1024, 6144], P('expert', 'tensor'), may hold values from -0.1875 to 0.1875
Outputs:
- mixed: bfloat16 [1024, 6144], P(('groups', 'expert', 'tensor')), parts along dimension 0
The draws below stay inside these ranges and needn't reach their ends.
There are 2 independent parts, one for each index of `groups`. The reference program is written for one: setup_inputs(seed, part) draws one part's arguments, and reference() takes and returns one part's arrays. A program takes and returns all parts, laid end to end along the dimension named above; an argument that names none is the same for every part. Nothing has to cross between parts.
Inputs may be any that keep to these rules, and one draw needn't show every extreme that they name: `expert_ids`: each token names 2 different experts. Within the 32 tokens of one device, no expert is named more than 32 times, a bound that some block reaches.
All inputs are finite; a program needn't handle non-finite values.
Results may differ from the reference program's by a relative error of at most 0.011.
Values may be sent and summed in bfloat16 or wider, within the bound.
No kernel may reach another device: no remote copies, remote signals or barrier semaphores. Data moves between devices by JAX's collectives and lax.ppermute only.
A program may use at most 64 MiB of HBM per device.

```python
import math
import jax
import jax.numpy as jnp
import numpy as np
from jax import lax

D = 6144
FF = 1024
TOP = 2
TOK_DEV = 32
EXPERTS = 4
CAP = 32
TOKENS = 512
N_TENSOR = 4


def block_scale(rng, dims, split, low, high):
    loudness, own = 1.0, jax.random.fold_in(rng, 6)
    for position, parts in split:
        draws = jnp.exp(jax.random.uniform(jax.random.fold_in(own, position), (parts,), jnp.float32, low / len(split), high / len(split)))
        loudness = loudness * jnp.repeat(draws, dims[position] // parts).reshape([-1 if axis == position else 1 for axis in range(len(dims))])
    return loudness


def shared_out(rng, own, number, rows, amount, top, limit, slope):
    sequence = jax.random.permutation(rng, amount)
    heavy_load, usual = portions_of(amount, rows * top, limit, slope, True), portions_of(amount, rows * top, limit, slope, False)
    places = jnp.arange(amount)

    def named(lengths, offset_by):
        used = int((lengths > 0).sum())
        fixed = max(1, used // 4)
        moved = fixed + (places - fixed + offset_by * (used - fixed)) % max(1, amount - fixed)
        return jnp.zeros((amount,), jnp.int32).at[sequence[jnp.where(places < fixed, places, moved)]].set(jnp.asarray(lengths, jnp.int32))

    lengths = jnp.where(number % 4 == 0, named(heavy_load, number // 4), named(usual, number - number // 4 - 1))
    mixed = jax.random.permutation(jax.random.fold_in(own, 3), amount)
    giver, sink = mixed[0:amount // 2 * 2:2], mixed[1:amount // 2 * 2:2]
    room = jnp.minimum(lengths[giver] - 1, limit - lengths[sink]) // 2
    room = jnp.where((giver == sequence[0]) | (sink == sequence[0]) | (lengths[sink] == 0), 0, jnp.maximum(room, 0))
    moved = jax.random.randint(jax.random.fold_in(own, 4), (amount // 2,), 0, 1 << 20) % (room + 1)
    lengths = lengths.at[giver].add(-moved).at[sink].add(moved)
    members = jnp.searchsorted(jnp.cumsum(lengths), jnp.arange(rows * top), side="right").astype(jnp.int32)
    listing = members.reshape(top, rows).T
    listing = listing[jax.random.permutation(jax.random.fold_in(own, 1), rows)]
    offset_by = jax.random.randint(jax.random.fold_in(own, 2), (rows, 1), 0, top)
    return jnp.take_along_axis(listing, (jnp.arange(top)[None, :] + offset_by) % top, axis=1)


def portions_of(count, total, most, skew, full):
    portions = [(1 << 20) // math.isqrt(standing ** skew) + 1 for standing in range(1, count + 1)]
    largest = most if full else min(most, max(-(-total // count), total * portions[0] // sum(portions)))
    least = 1 if total - largest >= count - 1 else 0
    holding, rest = [largest] + [least] * (count - 1), total - largest - least * (count - 1)
    while rest > 0:
        movable = [i for i in range(1, count) if holding[i] < largest] or [i for i in range(1, count) if holding[i] < most]
        whole, budget = sum([portions[i] for i in movable]), rest
        for i in movable:
            more = min(most - holding[i], max(1, budget * portions[i] // whole), rest)
            holding[i] = holding[i] + more
            rest = rest - more
    return np.array(holding)


def noise(key, extent, scale, limit, pieces=(), held_as=jnp.bfloat16):
    drawn = jax.random.normal(key, extent, jnp.float32) * scale
    if len(pieces) > 0:
        drawn = block_scale(key, extent, pieces, -0.22, 0.18) * drawn
    return jnp.clip(drawn, min=-limit, max=limit).astype(held_as)


def setup_inputs(seed: int = 0, part: int = 0) -> dict:
    key_list = jax.random.split(jax.random.key(seed), 8)
    part_splits = jax.random.split(jax.random.fold_in(key_list[7], part), 8)
    tokens = noise(part_splits[0], (TOKENS, D), 1.0, 6.0, ((0, 16),))
    expert_ids_keys = jax.random.split(jax.random.fold_in(part_splits[1], 1), TOKENS // TOK_DEV)
    expert_ids_turns = jax.random.permutation(jax.random.fold_in(part_splits[1], 3), TOKENS // TOK_DEV)
    expert_ids = jax.vmap(lambda own, number: shared_out(jax.random.fold_in(part_splits[1], 2), own, number, TOK_DEV, EXPERTS, TOP, CAP, 2))(expert_ids_keys, expert_ids_turns).reshape((TOKENS, TOP))
    gate_scores = jnp.clip(0.1 + 0.9 * jax.random.uniform(part_splits[2], (TOKENS, TOP), jnp.float32) ** block_scale(part_splits[2], (TOKENS, TOP), ((0, 16),), -0.2, 0.2), 0.1, 1.0)
    norm_gain = jnp.clip(1.0 + 0.18 * jax.random.normal(key_list[3], (D,), jnp.float32), 0.1, 1.9)
    w_gate = noise(key_list[4], (EXPERTS, D, FF), D ** -0.5, 0.078125, ((0, 4), (2, 4)))
    w_up = noise(key_list[5], (EXPERTS, D, FF), D ** -0.5, 0.078125, ((0, 4), (2, 4)))
    w_down = noise(key_list[6], (EXPERTS, FF, D), FF ** -0.5, 0.1875, ((0, 4), (1, 4)))
    return {"tokens": tokens, "expert_ids": expert_ids, "gate_scores": gate_scores, "norm_gain": norm_gain, "w_gate": w_gate, "w_up": w_up, "w_down": w_down}


def reference(tokens, expert_ids, gate_scores, norm_gain, w_gate, w_up, w_down):
    values = tokens.astype(jnp.float32)
    scale = lax.rsqrt(lax.optimization_barrier(jnp.mean(values * values, axis=-1, keepdims=True)) + 1e-05)
    normed = (values * scale * norm_gain).astype(jnp.bfloat16)
    blocks = TOKENS // TOK_DEV
    assigned = TOK_DEV * TOP
    block_ids = expert_ids.reshape(blocks, assigned).astype(jnp.int32)
    onehot = (block_ids[:, :, None] == jnp.arange(EXPERTS, dtype=jnp.int32)[None, None, :]).astype(jnp.int32)
    earlier = jnp.cumsum(onehot, axis=1) - onehot
    slot = lax.optimization_barrier(jnp.sum(earlier * onehot, axis=-1)).astype(jnp.int32)
    target = (block_ids * CAP + slot).astype(jnp.int32)
    repeated = jnp.repeat(normed.reshape(blocks, TOK_DEV, D), TOP, axis=1)
    block_index = jnp.broadcast_to(jnp.arange(blocks, dtype=jnp.int32)[:, None], (blocks, assigned))
    buffer = jnp.zeros((blocks, EXPERTS * CAP, D), jnp.bfloat16).at[block_index, target].set(repeated)
    per_expert = buffer.reshape(blocks, EXPERTS, CAP, D).transpose(1, 0, 2, 3).reshape(EXPERTS, blocks * CAP, D)
    group = FF // N_TENSOR

    def expert_fn(operands):
        rows, gate_w, up_w, down_w = operands
        gate = jnp.dot(rows, gate_w, preferred_element_type=jnp.float32)
        up = jnp.dot(rows, up_w, preferred_element_type=jnp.float32)
        hidden = (jax.nn.silu(gate) * up).astype(jnp.bfloat16)
        total = jnp.zeros((rows.shape[0], D), jnp.float32)
        for index in range(N_TENSOR):
            part = jnp.dot(hidden[:, index * group:(index + 1) * group], down_w[index * group:(index + 1) * group], preferred_element_type=jnp.float32)
            total = total + part.astype(jnp.bfloat16).astype(jnp.float32)
        return total.astype(jnp.bfloat16)
    outputs = lax.map(expert_fn, (per_expert, w_gate, w_up, w_down))
    back = outputs.reshape(EXPERTS, blocks, CAP, D).transpose(1, 0, 2, 3).reshape(blocks, EXPERTS * CAP, D)
    picked = jnp.take_along_axis(back, target[:, :, None], axis=1).astype(jnp.float32)
    picked = picked.reshape(TOKENS, TOP, D)
    mixed = lax.optimization_barrier(jnp.sum(gate_scores[:, :, None] * picked, axis=1))
    return mixed.astype(jnp.bfloat16)
```

```python
import functools

import jax
import jax.numpy as jnp
from jax import lax
from jax.experimental import pallas as pl
from jax.experimental.pallas import tpu as pltpu
from jax.sharding import PartitionSpec as P

LANES = 128


def routed(tokens, expert_ids, gate_scores, norm_gain, w_gate, w_up, w_down):
    rows = tokens.shape[0]
    width = tokens.shape[1]
    picks = expert_ids.shape[1]
    experts = lax.axis_size("expert")
    capacity = 4 * rows // experts
    values = tokens.astype(jnp.float32)
    scale = lax.rsqrt(jnp.mean(values * values, axis=-1, keepdims=True) + 1e-05)
    normed = (values * scale * norm_gain).astype(jnp.bfloat16)
    flat_ids = expert_ids.reshape(-1)
    onehot = (flat_ids[:, None] == jnp.arange(experts, dtype=jnp.int32)[None, :]).astype(jnp.int32)
    earlier = jnp.cumsum(onehot, axis=0) - onehot
    slot = jnp.sum(earlier * onehot, axis=1)
    target = flat_ids * capacity + slot
    placing = jnp.arange(experts * capacity, dtype=jnp.int32)[:, None] == target[None, :]
    placing = placing.reshape(experts * capacity, rows, picks)
    place_tok = jnp.sum(placing.astype(jnp.float32), axis=2).astype(jnp.bfloat16)
    weighting = jnp.sum(placing.astype(jnp.float32) * gate_scores[None, :, :], axis=2)
    outgoing = jnp.dot(place_tok, normed, preferred_element_type=jnp.float32).astype(jnp.bfloat16)
    outgoing = outgoing.reshape(experts, capacity, width)
    arrived = lax.all_to_all(outgoing, "expert", split_axis=0, concat_axis=0, tiled=True)
    arrived = arrived.reshape(-1, width)
    piece = lax.all_gather(arrived, "tensor", axis=0, tiled=True)
    gate = jnp.dot(piece, w_gate[0], preferred_element_type=jnp.float32)
    up = jnp.dot(piece, w_up[0], preferred_element_type=jnp.float32)
    hidden = (jax.nn.silu(gate) * up).astype(jnp.bfloat16)
    parts = jnp.dot(hidden, w_down[0], preferred_element_type=jnp.float32)
    summed = lax.psum_scatter(parts.astype(jnp.bfloat16), "tensor", scatter_dimension=0, tiled=True)
    summed = summed.reshape(experts, capacity, width)
    results = lax.all_to_all(summed, "expert", split_axis=0, concat_axis=0, tiled=True)
    results = results.reshape(experts * capacity, width)
    mixed = jnp.dot(
        weighting.T,
        results.astype(jnp.float32),
        precision=lax.Precision.HIGHEST,
        preferred_element_type=jnp.float32,
    )
    return mixed.astype(jnp.bfloat16)


def norm_body(experts, tok_ref, ids_ref, score_ref, gain_ref, out_ref):
    rows, width = tok_ref.shape
    values = tok_ref[...].astype(jnp.float32)
    scale = lax.rsqrt(jnp.mean(values * values, axis=-1, keepdims=True) + 1e-05)
    out_ref[:, :width] = (values * scale * gain_ref[...]).astype(jnp.bfloat16)
    lane = lax.broadcasted_iota(jnp.int32, (rows, LANES), 1)
    expert = lax.rem(lane, experts)
    weight = jnp.zeros((rows, LANES), jnp.float32)
    for k in range(ids_ref.shape[1]):
        weight += jnp.where(ids_ref[:, k:k + 1] == expert, score_ref[:, k:k + 1], 0.0)
    high = weight.astype(jnp.bfloat16).astype(jnp.float32)
    rest = weight - high
    middle = rest.astype(jnp.bfloat16).astype(jnp.float32)
    low = rest - middle
    term = jnp.where(lane < experts, high, jnp.where(lane < 2 * experts, middle, low))
    out_ref[:, width:] = jnp.where(lane < 3 * experts, term, 0.0).astype(jnp.bfloat16)


def expert_call(me, blocks, gate, up, down, experts):
    rows, width = blocks[0].shape[0], down.shape[1]
    one = jax.ShapeDtypeStruct((rows, width), jnp.bfloat16)
    vmem = pl.BlockSpec(memory_space=pltpu.VMEM)
    return pl.pallas_call(
        functools.partial(expert_body, experts, 1024),
        out_shape=[one, one, jax.ShapeDtypeStruct((2 * rows, width), jnp.bfloat16)],
        in_specs=[pl.BlockSpec(memory_space=pltpu.SMEM)] + [vmem] * (len(blocks) + 3),
        out_specs=[vmem] * 3,
        compiler_params=pltpu.CompilerParams(vmem_limit_bytes=24 << 20),
        cost_estimate=pl.CostEstimate(
            flops=6 * len(blocks) * rows * width * gate.shape[1], bytes_accessed=16 << 20, transcendentals=0),
    )(me, *blocks, gate, up, down)


def expert_body(experts, step, me_ref, *refs):
    ins, outs = refs[:-3], refs[-3:]
    blocks, (gate_ref, up_ref, down_ref) = ins[:-3], ins[-3:]
    width, rows = down_ref.shape[1], blocks[0].shape[0]
    gate = up = None
    for k in range(0, width, step):
        part = jnp.concatenate([b[:, k:k + step] for b in blocks], axis=0)
        g = jnp.dot(part, gate_ref[k:k + step, :], preferred_element_type=jnp.float32)
        u = jnp.dot(part, up_ref[k:k + step, :], preferred_element_type=jnp.float32)
        gate = g if gate is None else gate + g
        up = u if up is None else up + u
    terms = jnp.concatenate([b[:, width:] for b in blocks], axis=0).astype(jnp.float32)
    lane = lax.broadcasted_iota(jnp.int32, terms.shape, 1)
    weight = jnp.sum(jnp.where(lax.rem(lane, experts) == me_ref[0], terms, 0.0), axis=1, keepdims=True)
    hidden = gate / (1.0 + jnp.exp(-gate)) * up * weight
    hidden = jnp.where(weight == 0.0, 0.0, hidden).astype(jnp.bfloat16)
    for n in range(0, width, step):
        part = jnp.dot(hidden, down_ref[:, n:n + step], preferred_element_type=jnp.float32).astype(jnp.bfloat16)
        outs[0][:, n:n + step] = part[:rows]
        outs[1][:, n:n + step] = part[rows:2 * rows]
        outs[2][:, n:n + step] = part[2 * rows:]


def gathered(tokens, expert_ids, gate_scores, norm_gain, w_gate, w_up, w_down):
    rows, width = tokens.shape
    experts, slices = lax.axis_size("expert"), lax.axis_size("tensor")
    vmem = pl.BlockSpec(memory_space=pltpu.VMEM)
    own = pl.pallas_call(
        functools.partial(norm_body, experts),
        out_shape=jax.ShapeDtypeStruct((rows, width + LANES), jnp.bfloat16),
        in_specs=[vmem] * 4,
        out_specs=vmem,
        compiler_params=pltpu.CompilerParams(vmem_limit_bytes=8 << 20),
    )(tokens, expert_ids, gate_scores, norm_gain.reshape(1, width))
    me = lax.axis_index("expert").astype(jnp.int32).reshape(1)

    def swap(array, bit):
        return lax.ppermute(array, "tensor", [(i, i ^ bit) for i in range(slices)])

    def turn(array):
        return lax.ppermute(array, "expert", [(i, (i + 1) % experts) for i in range(experts)])

    def add(a, b):
        return (a.astype(jnp.float32) + b.astype(jnp.float32)).astype(jnp.bfloat16)

    held = [own]
    for _ in range(experts - 1):
        held.append(turn(held[-1]))
    sums = []
    for block in held:
        far = swap(block, 2)
        blocks = [block, far, swap(block, 1), swap(far, 1)]
        mine, other, sibling = expert_call(me, blocks, w_gate[0], w_up[0], w_down[0], experts)
        back = swap(sibling, 1)
        other = add(other, back[rows:])
        mine = add(mine, back[:rows])
        sums.append(add(mine, swap(other, 2)))
    total = sums[1]
    for s in list(sums[2:]) + [sums[0]]:
        total = add(turn(total), s)
    return total


def on_device(tokens, expert_ids, *rest):
    experts, slices = lax.axis_size("expert"), lax.axis_size("tensor")
    dense = 4 * tokens.shape[0] // experts >= tokens.shape[0]
    plan = gathered if dense and slices == 4 and experts > 1 and 3 * experts <= LANES else routed
    return plan(tokens, expert_ids, *rest)


def solution(mesh):
    return jax.shard_map(
        on_device,
        mesh=mesh,
        in_specs=(
            P(("groups", "expert", "tensor"), None),
            P(("groups", "expert", "tensor"), None),
            P(("groups", "expert", "tensor"), None),
            P(),
            P("expert", None, "tensor"),
            P("expert", None, "tensor"),
            P("expert", "tensor", None),
        ),
        out_specs=P(("groups", "expert", "tensor"), None),
        check_vma=False,
    )
```

```python
import functools

import jax
import jax.numpy as jnp
from jax import lax
from jax.experimental import pallas as pl
from jax.experimental.pallas import tpu as pltpu
from jax.sharding import PartitionSpec as P


LANES = 128
STEP = 1024


def routed(tokens, expert_ids, gate_scores, norm_gain, w_gate, w_up, w_down):
    rows = tokens.shape[0]
    width = tokens.shape[1]
    picks = expert_ids.shape[1]
    experts = lax.axis_size("expert")
    capacity = 4 * rows // experts
    values = tokens.astype(jnp.float32)
    scale = lax.rsqrt(jnp.mean(values * values, axis=-1, keepdims=True) + 1e-05)
    normed = (values * scale * norm_gain).astype(jnp.bfloat16)
    flat_ids = expert_ids.reshape(-1)
    onehot = (flat_ids[:, None] == jnp.arange(experts, dtype=jnp.int32)[None, :]).astype(jnp.int32)
    earlier = jnp.cumsum(onehot, axis=0) - onehot
    slot = jnp.sum(earlier * onehot, axis=1)
    target = flat_ids * capacity + slot
    placing = jnp.arange(experts * capacity, dtype=jnp.int32)[:, None] == target[None, :]
    placing = placing.reshape(experts * capacity, rows, picks)
    place_tok = jnp.sum(placing.astype(jnp.float32), axis=2).astype(jnp.bfloat16)
    weighting = jnp.sum(placing.astype(jnp.float32) * gate_scores[None, :, :], axis=2)
    outgoing = jnp.dot(place_tok, normed, preferred_element_type=jnp.float32).astype(jnp.bfloat16)
    outgoing = outgoing.reshape(experts, capacity, width)
    arrived = lax.all_to_all(outgoing, "expert", split_axis=0, concat_axis=0, tiled=True)
    arrived = arrived.reshape(-1, width)
    piece = lax.all_gather(arrived, "tensor", axis=0, tiled=True)
    gate = jnp.dot(piece, w_gate[0], preferred_element_type=jnp.float32)
    up = jnp.dot(piece, w_up[0], preferred_element_type=jnp.float32)
    hidden = (jax.nn.silu(gate) * up).astype(jnp.bfloat16)
    parts = jnp.dot(hidden, w_down[0], preferred_element_type=jnp.float32)
    summed = lax.psum_scatter(parts.astype(jnp.bfloat16), "tensor", scatter_dimension=0, tiled=True)
    summed = summed.reshape(experts, capacity, width)
    results = lax.all_to_all(summed, "expert", split_axis=0, concat_axis=0, tiled=True)
    results = results.reshape(experts * capacity, width)
    mixed = jnp.dot(
        weighting.T,
        results.astype(jnp.float32),
        precision=lax.Precision.HIGHEST,
        preferred_element_type=jnp.float32,
    )
    return mixed.astype(jnp.bfloat16)


def norm_body(experts, tok_hbm, ids_hbm, score_hbm, gain_hbm, out_ref, tok_ref, ids_ref, score_ref, gain_ref, sems):
    pairs = [(ids_hbm, ids_ref), (score_hbm, score_ref), (tok_hbm, tok_ref), (gain_hbm, gain_ref)]
    copies = [pltpu.make_async_copy(src, dst, sems.at[i]) for i, (src, dst) in enumerate(pairs)]
    for copy in copies:
        copy.start()
    rows, width = tok_ref.shape
    copies[0].wait()
    copies[1].wait()
    lane = lax.broadcasted_iota(jnp.int32, (rows, LANES), 1)
    expert = lax.rem(lane, experts).astype(jnp.float32)
    square = (rows, rows)
    diagonal = lax.broadcasted_iota(jnp.int32, square, 0) == lax.broadcasted_iota(jnp.int32, square, 1)

    def column(row):
        return jnp.sum(jnp.where(diagonal, jnp.broadcast_to(row, square), 0.0), axis=1, keepdims=True)

    weight = jnp.zeros((rows, LANES), jnp.float32)
    for k in range(ids_ref.shape[0]):
        chosen = column(ids_ref[k:k + 1, :].astype(jnp.float32))
        weight += jnp.where(chosen == expert, column(score_ref[k:k + 1, :]), 0.0)
    high = weight.astype(jnp.bfloat16).astype(jnp.float32)
    rest = weight - high
    middle = rest.astype(jnp.bfloat16).astype(jnp.float32)
    low = rest - middle
    term = jnp.where(lane < experts, high, jnp.where(lane < 2 * experts, middle, low))
    out_ref[:, width:] = jnp.where(lane < 3 * experts, term, 0.0).astype(jnp.bfloat16)
    copies[2].wait()
    values = tok_ref[...].astype(jnp.float32)
    scale = lax.rsqrt(jnp.mean(values * values, axis=-1, keepdims=True) + 1e-05)
    copies[3].wait()
    out_ref[:, :width] = (values * scale * gain_ref[...]).astype(jnp.bfloat16)


def norm_call(tokens, expert_ids, gate_scores, norm_gain, experts):
    rows, width = tokens.shape
    operands = (tokens, expert_ids.T, gate_scores.T, norm_gain.reshape(1, width))
    operands = [pltpu.with_memory_space_constraint(o, pltpu.HBM) for o in operands]
    return pl.pallas_call(
        functools.partial(norm_body, experts),
        out_shape=jax.ShapeDtypeStruct((rows, width + LANES), jnp.bfloat16),
        in_specs=[pl.BlockSpec(memory_space=pltpu.HBM)] * 4,
        out_specs=pl.BlockSpec(memory_space=pltpu.VMEM),
        scratch_shapes=[pltpu.VMEM(o.shape, o.dtype) for o in operands] + [pltpu.SemaphoreType.DMA((4,))],
        compiler_params=pltpu.CompilerParams(vmem_limit_bytes=4 << 20),
    )(*operands)


def expert_call(me, blocks, weights, experts, fetch):
    rows, width = blocks[0].shape[0], weights[2].shape[1]
    pieces = width // STEP
    one = jax.ShapeDtypeStruct((rows, width), jnp.bfloat16)
    vmem = pl.BlockSpec(memory_space=pltpu.VMEM)
    held = pl.BlockSpec(memory_space=pltpu.HBM) if fetch else vmem
    if fetch:
        weights = [pltpu.with_memory_space_constraint(w, pltpu.HBM) for w in weights]
    scratch = [pltpu.VMEM(w.shape, w.dtype) for w in weights] + [pltpu.SemaphoreType.DMA((3, pieces))]
    return pl.pallas_call(
        functools.partial(expert_body, experts, fetch),
        out_shape=[one, one, jax.ShapeDtypeStruct((2 * rows, width), jnp.bfloat16)],
        in_specs=[pl.BlockSpec(memory_space=pltpu.SMEM)] + [vmem] * len(blocks) + [held] * 3,
        out_specs=[vmem] * 3,
        scratch_shapes=scratch if fetch else [],
        compiler_params=pltpu.CompilerParams(vmem_limit_bytes=20 << 20),
        cost_estimate=pl.CostEstimate(
            flops=6 * len(blocks) * rows * width * weights[0].shape[1], bytes_accessed=16 << 20, transcendentals=0),
    )(me, *blocks, *weights)


def expert_body(experts, fetch, me_ref, *refs):
    blocks, refs = refs[:4], refs[4:]
    stored, outs = refs[:3], refs[3:6]
    width, rows = stored[2].shape[1], blocks[0].shape[0]
    pieces = [pl.ds(k, STEP) for k in range(0, width, STEP)]
    gate_ref, up_ref, down_ref = refs[6:9] if fetch else stored

    def copy(which, i):
        at = (slice(None), pieces[i]) if which == 2 else (pieces[i], slice(None))
        return pltpu.make_async_copy(stored[which].at[at], refs[6 + which].at[at], refs[9].at[which, i])

    def ready(which, i):
        if fetch:
            copy(which, i).wait()

    if fetch:
        for i in range(len(pieces)):
            copy(0, i).start()
            copy(1, i).start()
        for i in range(len(pieces)):
            copy(2, i).start()
    gate = up = None
    for i, piece in enumerate(pieces):
        part = jnp.concatenate([b[:, piece] for b in blocks], axis=0)
        ready(0, i)
        g = jnp.dot(part, gate_ref[piece, :], preferred_element_type=jnp.float32)
        ready(1, i)
        u = jnp.dot(part, up_ref[piece, :], preferred_element_type=jnp.float32)
        gate = g if gate is None else gate + g
        up = u if up is None else up + u
    terms = jnp.concatenate([b[:, width:] for b in blocks], axis=0).astype(jnp.float32)
    lane = lax.broadcasted_iota(jnp.int32, terms.shape, 1)
    weight = jnp.sum(jnp.where(lax.rem(lane, experts) == me_ref[0], terms, 0.0), axis=1, keepdims=True)
    hidden = gate / (1.0 + jnp.exp(-gate)) * up * weight
    hidden = jnp.where(weight == 0.0, 0.0, hidden).astype(jnp.bfloat16)
    for i, piece in enumerate(pieces):
        ready(2, i)
        part = jnp.dot(hidden, down_ref[:, piece], preferred_element_type=jnp.float32).astype(jnp.bfloat16)
        outs[0][:, piece] = part[:rows]
        outs[1][:, piece] = part[rows:2 * rows]
        outs[2][:, piece] = part[2 * rows:]


def gathered(tokens, expert_ids, gate_scores, norm_gain, w_gate, w_up, w_down):
    rows = tokens.shape[0]
    experts, slices = lax.axis_size("expert"), lax.axis_size("tensor")
    me = lax.axis_index("expert").astype(jnp.int32).reshape(1)

    def swap(array, bit):
        return lax.ppermute(array, "tensor", [(i, i ^ bit) for i in range(slices)])

    def turn(array):
        return lax.ppermute(array, "expert", [(i, (i + 1) % experts) for i in range(experts)])

    def add(a, b):
        return (a.astype(jnp.float32) + b.astype(jnp.float32)).astype(jnp.bfloat16)

    own = norm_call(tokens, expert_ids, gate_scores, norm_gain, experts)
    weights = (w_gate[0], w_up[0], w_down[0])
    near = [own]
    for _ in range(1, experts):
        near.append(turn(near[-1]))
    far = [swap(near[s], 2) for s in range(experts - 1)]
    far.append(turn(far[-1]))
    sums = []
    for s in range(experts):
        blocks = [near[s], far[s], swap(near[s], 1), swap(far[s], 1)]
        mine, other, sibling = expert_call(me, blocks, weights, experts, s == 0)
        back = swap(sibling, 1)
        other = add(other, back[rows:])
        mine = add(mine, back[:rows])
        sums.append(add(mine, swap(other, 2)))
    total = sums[1]
    for s in range(2, experts + 1):
        total = add(turn(total), sums[s % experts])
    return total


def is_dense(mesh_shape, rows):
    experts, slices = mesh_shape["expert"], mesh_shape["tensor"]
    return 4 * rows // experts >= rows and slices == 4 and experts > 2 and 3 * experts <= LANES


def on_device(tokens, *rest):
    shape = {name: lax.axis_size(name) for name in ("expert", "tensor")}
    plan = gathered if is_dense(shape, tokens.shape[0]) else routed
    return plan(tokens, *rest)


def solution(mesh):
    return jax.shard_map(
        on_device,
        mesh=mesh,
        in_specs=(
            P(("groups", "expert", "tensor"), None),
            P(("groups", "expert", "tensor"), None),
            P(("groups", "expert", "tensor"), None),
            P(),
            P("expert", None, "tensor"),
            P("expert", None, "tensor"),
            P("expert", "tensor", None),
        ),
        out_specs=P(("groups", "expert", "tensor"), None),
        check_vma=False,
    )
```

```python
import functools

import jax
import jax.numpy as jnp
from jax import lax
from jax.experimental import pallas as pl
from jax.experimental.pallas import tpu as pltpu
from jax.sharding import PartitionSpec as P


LANES = 128
STEP = 1024
PARTS = 2


def routed(tokens, expert_ids, gate_scores, norm_gain, w_gate, w_up, w_down):
    rows = tokens.shape[0]
    width = tokens.shape[1]
    picks = expert_ids.shape[1]
    experts = lax.axis_size("expert")
    capacity = 4 * rows // experts
    values = tokens.astype(jnp.float32)
    scale = lax.rsqrt(jnp.mean(values * values, axis=-1, keepdims=True) + 1e-05)
    normed = (values * scale * norm_gain).astype(jnp.bfloat16)
    flat_ids = expert_ids.reshape(-1)
    onehot = (flat_ids[:, None] == jnp.arange(experts, dtype=jnp.int32)[None, :]).astype(jnp.int32)
    earlier = jnp.cumsum(onehot, axis=0) - onehot
    slot = jnp.sum(earlier * onehot, axis=1)
    target = flat_ids * capacity + slot
    placing = jnp.arange(experts * capacity, dtype=jnp.int32)[:, None] == target[None, :]
    placing = placing.reshape(experts * capacity, rows, picks)
    place_tok = jnp.sum(placing.astype(jnp.float32), axis=2).astype(jnp.bfloat16)
    weighting = jnp.sum(placing.astype(jnp.float32) * gate_scores[None, :, :], axis=2)
    outgoing = jnp.dot(place_tok, normed, preferred_element_type=jnp.float32).astype(jnp.bfloat16)
    outgoing = outgoing.reshape(experts, capacity, width)
    arrived = lax.all_to_all(outgoing, "expert", split_axis=0, concat_axis=0, tiled=True)
    arrived = arrived.reshape(-1, width)
    piece = lax.all_gather(arrived, "tensor", axis=0, tiled=True)
    gate = jnp.dot(piece, w_gate[0], preferred_element_type=jnp.float32)
    up = jnp.dot(piece, w_up[0], preferred_element_type=jnp.float32)
    hidden = (jax.nn.silu(gate) * up).astype(jnp.bfloat16)
    parts = jnp.dot(hidden, w_down[0], preferred_element_type=jnp.float32)
    summed = lax.psum_scatter(parts.astype(jnp.bfloat16), "tensor", scatter_dimension=0, tiled=True)
    summed = summed.reshape(experts, capacity, width)
    results = lax.all_to_all(summed, "expert", split_axis=0, concat_axis=0, tiled=True)
    results = results.reshape(experts * capacity, width)
    mixed = jnp.dot(
        weighting.T,
        results.astype(jnp.float32),
        precision=lax.Precision.HIGHEST,
        preferred_element_type=jnp.float32,
    )
    return mixed.astype(jnp.bfloat16)


def norm_body(experts, tok_hbm, ids_hbm, score_hbm, gain_hbm, *refs):
    outs, (tok_ref, ids_ref, score_ref, gain_ref, sems) = refs[:-5], refs[-5:]
    pairs = [(ids_hbm, ids_ref), (score_hbm, score_ref), (tok_hbm, tok_ref), (gain_hbm, gain_ref)]
    copies = [pltpu.make_async_copy(src, dst, sems.at[i]) for i, (src, dst) in enumerate(pairs)]
    for copy in copies:
        copy.start()
    rows, width = tok_ref.shape
    copies[0].wait()
    copies[1].wait()
    lane = lax.broadcasted_iota(jnp.int32, (rows, LANES), 1)
    expert = lax.rem(lane, experts).astype(jnp.float32)
    square = (rows, rows)
    diagonal = lax.broadcasted_iota(jnp.int32, square, 0) == lax.broadcasted_iota(jnp.int32, square, 1)

    def column(row):
        return jnp.sum(jnp.where(diagonal, jnp.broadcast_to(row, square), 0.0), axis=1, keepdims=True)

    weight = jnp.zeros((rows, LANES), jnp.float32)
    for k in range(ids_ref.shape[0]):
        chosen = column(ids_ref[k:k + 1, :].astype(jnp.float32))
        weight += jnp.where(chosen == expert, column(score_ref[k:k + 1, :]), 0.0)
    high = weight.astype(jnp.bfloat16).astype(jnp.float32)
    rest = weight - high
    middle = rest.astype(jnp.bfloat16).astype(jnp.float32)
    low = rest - middle
    term = jnp.where(lane < experts, high, jnp.where(lane < 2 * experts, middle, low))
    term = jnp.where(lane < 3 * experts, term, 0.0).astype(jnp.bfloat16)
    part = rows // len(outs)
    for i, out_ref in enumerate(outs):
        out_ref[:, width:] = term[i * part:(i + 1) * part]
    copies[2].wait()
    values = tok_ref[...].astype(jnp.float32)
    scale = lax.rsqrt(jnp.mean(values * values, axis=-1, keepdims=True) + 1e-05)
    copies[3].wait()
    normed = (values * scale * gain_ref[...]).astype(jnp.bfloat16)
    for i, out_ref in enumerate(outs):
        out_ref[:, :width] = normed[i * part:(i + 1) * part]


def norm_call(tokens, expert_ids, gate_scores, norm_gain, experts):
    rows, width = tokens.shape
    operands = (tokens, expert_ids.T, gate_scores.T, norm_gain.reshape(1, width))
    operands = [pltpu.with_memory_space_constraint(o, pltpu.HBM) for o in operands]
    return pl.pallas_call(
        functools.partial(norm_body, experts),
        out_shape=[jax.ShapeDtypeStruct((rows // PARTS, width + LANES), jnp.bfloat16)] * PARTS,
        in_specs=[pl.BlockSpec(memory_space=pltpu.HBM)] * 4,
        out_specs=[pl.BlockSpec(memory_space=pltpu.VMEM)] * PARTS,
        scratch_shapes=[pltpu.VMEM(o.shape, o.dtype) for o in operands] + [pltpu.SemaphoreType.DMA((4,))],
        compiler_params=pltpu.CompilerParams(vmem_limit_bytes=4 << 20),
    )(*operands)


def load_body(*refs):
    count = (len(refs) - 1) // 2
    copies = [pltpu.make_async_copy(refs[i], refs[count + i], refs[-1].at[i]) for i in range(count)]
    for copy in copies:
        copy.start()
    for copy in copies:
        copy.wait()


def load_call(*arrays):
    vmem = pl.BlockSpec(memory_space=pltpu.VMEM)
    return pl.pallas_call(
        load_body,
        out_shape=[jax.ShapeDtypeStruct(a.shape, a.dtype) for a in arrays],
        in_specs=[pl.BlockSpec(memory_space=pltpu.HBM)] * len(arrays),
        out_specs=[vmem] * len(arrays),
        scratch_shapes=[pltpu.SemaphoreType.DMA((len(arrays),))],
        compiler_params=pltpu.CompilerParams(vmem_limit_bytes=12 << 20),
    )(*[pltpu.with_memory_space_constraint(a, pltpu.HBM) for a in arrays])


def pack_body(*refs):
    part = refs[0].shape[0]
    for i, ref in enumerate(refs[:-1]):
        refs[-1][i * part:(i + 1) * part, :] = ref[...]


def pack_call(arrays):
    rows, width = arrays[0].shape
    vmem = pl.BlockSpec(memory_space=pltpu.VMEM)
    return pl.pallas_call(
        pack_body,
        out_shape=jax.ShapeDtypeStruct((len(arrays) * rows, width), arrays[0].dtype),
        in_specs=[vmem] * len(arrays),
        out_specs=vmem,
        compiler_params=pltpu.CompilerParams(vmem_limit_bytes=4 << 20),
    )(*arrays)


def total_body(ins, outs, *refs):
    for out, terms in enumerate(outs):
        target = refs[ins + out] if len(refs) > ins + 1 else refs[ins].at[terms[-1]]
        value = None
        for which, at in terms[:-1]:
            term = refs[which][at, :].astype(jnp.float32)
            value = term if value is None else value + term
        target[...] = value.astype(jnp.bfloat16)


def total_call(arrays, outs, whole=False):
    part = min(a.shape[0] for a in arrays)
    width = arrays[0].shape[1]
    vmem = pl.BlockSpec(memory_space=pltpu.VMEM)
    plan = [[(w, pl.ds(r, part)) for w, r in terms] + [pl.ds(i * part, part)] for i, terms in enumerate(outs)]
    shape = jax.ShapeDtypeStruct((part * (len(outs) if whole else 1), width), jnp.bfloat16)
    return pl.pallas_call(
        functools.partial(total_body, len(arrays), plan),
        out_shape=[shape] * (1 if whole else len(outs)),
        in_specs=[vmem] * len(arrays),
        out_specs=[vmem] * (1 if whole else len(outs)),
        compiler_params=pltpu.CompilerParams(vmem_limit_bytes=4 << 20),
    )(*arrays)


def expert_call(blocks, weights, experts, rows):
    width = weights[2].shape[1]
    part = jax.ShapeDtypeStruct((rows // PARTS, width), jnp.bfloat16)
    vmem = pl.BlockSpec(memory_space=pltpu.VMEM)
    return pl.pallas_call(
        functools.partial(expert_body, experts),
        out_shape=[part] * (2 * PARTS) + [jax.ShapeDtypeStruct((2 * rows, width), jnp.bfloat16)],
        in_specs=[vmem] * (len(blocks) + 3),
        out_specs=[vmem] * (2 * PARTS + 1),
        compiler_params=pltpu.CompilerParams(vmem_limit_bytes=20 << 20),
        cost_estimate=pl.CostEstimate(
            flops=24 * rows * width * weights[0].shape[1], bytes_accessed=16 << 20, transcendentals=0),
    )(*blocks, *weights)


def expert_body(experts, *refs):
    blocks, (gate_ref, up_ref, down_ref), outs = refs[:2], refs[2:5], refs[5:]
    width = down_ref.shape[1]
    pieces = [pl.ds(k, STEP) for k in range(0, width, STEP)]

    gate = up = None
    for piece in pieces:
        part = jnp.concatenate([b[:, piece] for b in blocks], axis=0)
        g = jnp.dot(part, gate_ref[piece, :], preferred_element_type=jnp.float32)
        u = jnp.dot(part, up_ref[piece, :], preferred_element_type=jnp.float32)
        gate = g if gate is None else gate + g
        up = u if up is None else up + u
    terms = jnp.concatenate([b[:, width:] for b in blocks], axis=0).astype(jnp.float32)
    lane = lax.broadcasted_iota(jnp.int32, terms.shape, 1)
    weight = jnp.sum(jnp.where(lax.rem(lane, experts) == lax.axis_index("expert"), terms, 0.0), axis=1, keepdims=True)
    hidden = gate / (1.0 + jnp.exp(-gate)) * up * weight
    hidden = jnp.where(weight == 0.0, 0.0, hidden).astype(jnp.bfloat16)
    for piece in pieces:
        part = jnp.dot(hidden, down_ref[:, piece], preferred_element_type=jnp.float32).astype(jnp.bfloat16)
        row = 0
        for out in outs:
            out[:, piece] = part[row:row + out.shape[0]]
            row += out.shape[0]


def gathered(tokens, expert_ids, gate_scores, norm_gain, w_gate, w_up, w_down):
    rows = tokens.shape[0]
    experts, slices = lax.axis_size("expert"), lax.axis_size("tensor")

    def swap(arrays, bit):
        return send(arrays, "tensor", [(i, i ^ bit) for i in range(slices)])

    ring = list(range(0, experts, 2)) + list(range(1, experts, 2))[::-1]

    def turn(arrays):
        return send(arrays, "expert", [(ring[i - 1], ring[i]) for i in range(experts)])

    def send(arrays, axis, pairs):
        out = []
        for array in arrays:
            out.append(lax.ppermute(array, axis, pairs))
        return out

    own = list(norm_call(tokens, expert_ids, gate_scores, norm_gain, experts))
    weights = load_call(w_gate[0], w_up[0], w_down[0])
    near = [own]
    for _ in range(1, experts):
        near.append(turn(near[-1]))
    far = [swap(near[s], 2) for s in range(experts - 1)]
    far.append(turn(far[-1]))
    part = rows // PARTS
    sums = []
    for s in range(experts):
        here = pack_call(near[s] + far[s])
        there = swap([here], 1)
        *mine, sibling = expert_call([here, *there], weights, experts, rows)
        back = swap([sibling], 1)
        mine = total_call(mine + back, [[(i, 0), (2 * PARTS, i * part)] for i in range(2 * PARTS)])
        sums.append((mine[:PARTS], swap(mine[PARTS:], 2)))
    passed = [[] for _ in range(PARTS)]
    for s in range(1, experts):
        total = []
        for i in range(PARTS):
            terms = passed[i] + [sums[s][0][i], sums[s][1][i]]
            total += total_call(terms, [[(t, 0) for t in range(len(terms))]])
        passed = [[t] for t in turn(total)]
    terms = [t for i in range(PARTS) for t in passed[i] + [sums[0][0][i], sums[0][1][i]]]
    return total_call(terms, [[(3 * i + t, 0) for t in range(3)] for i in range(PARTS)], whole=True)[0]


def is_dense(mesh_shape, rows):
    experts, slices = mesh_shape["expert"], mesh_shape["tensor"]
    return 4 * rows // experts >= rows and slices == 4 and experts > 2 and 3 * experts <= LANES


def on_device(tokens, *rest):
    shape = {name: lax.axis_size(name) for name in ("expert", "tensor")}
    plan = gathered if is_dense(shape, tokens.shape[0]) else routed
    return plan(tokens, *rest)


def solution(mesh):
    return jax.shard_map(
        on_device,
        mesh=mesh,
        in_specs=(
            P(("groups", "expert", "tensor"), None),
            P(("groups", "expert", "tensor"), None),
            P(("groups", "expert", "tensor"), None),
            P(),
            P("expert", None, "tensor"),
            P("expert", None, "tensor"),
            P("expert", "tensor", None),
        ),
        out_specs=P(("groups", "expert", "tensor"), None),
        check_vma=False,
    )
```

```python
import functools

import jax
import jax.numpy as jnp
from jax import lax
from jax.experimental import pallas as pl
from jax.experimental.pallas import tpu as pltpu
from jax.sharding import PartitionSpec as P


LANES = 128
STEP = 1024
PARTS = 2


def routed(tokens, expert_ids, gate_scores, norm_gain, w_gate, w_up, w_down):
    rows = tokens.shape[0]
    width = tokens.shape[1]
    picks = expert_ids.shape[1]
    experts = lax.axis_size("expert")
    capacity = 4 * rows // experts
    values = tokens.astype(jnp.float32)
    scale = lax.rsqrt(jnp.mean(values * values, axis=-1, keepdims=True) + 1e-05)
    normed = (values * scale * norm_gain).astype(jnp.bfloat16)
    flat_ids = expert_ids.reshape(-1)
    onehot = (flat_ids[:, None] == jnp.arange(experts, dtype=jnp.int32)[None, :]).astype(jnp.int32)
    earlier = jnp.cumsum(onehot, axis=0) - onehot
    slot = jnp.sum(earlier * onehot, axis=1)
    target = flat_ids * capacity + slot
    placing = jnp.arange(experts * capacity, dtype=jnp.int32)[:, None] == target[None, :]
    placing = placing.reshape(experts * capacity, rows, picks)
    place_tok = jnp.sum(placing.astype(jnp.float32), axis=2).astype(jnp.bfloat16)
    weighting = jnp.sum(placing.astype(jnp.float32) * gate_scores[None, :, :], axis=2)
    outgoing = jnp.dot(place_tok, normed, preferred_element_type=jnp.float32).astype(jnp.bfloat16)
    outgoing = outgoing.reshape(experts, capacity, width)
    arrived = lax.all_to_all(outgoing, "expert", split_axis=0, concat_axis=0, tiled=True)
    arrived = arrived.reshape(-1, width)
    piece = lax.all_gather(arrived, "tensor", axis=0, tiled=True)
    gate = jnp.dot(piece, w_gate[0], preferred_element_type=jnp.float32)
    up = jnp.dot(piece, w_up[0], preferred_element_type=jnp.float32)
    hidden = (jax.nn.silu(gate) * up).astype(jnp.bfloat16)
    parts = jnp.dot(hidden, w_down[0], preferred_element_type=jnp.float32)
    summed = lax.psum_scatter(parts.astype(jnp.bfloat16), "tensor", scatter_dimension=0, tiled=True)
    summed = summed.reshape(experts, capacity, width)
    results = lax.all_to_all(summed, "expert", split_axis=0, concat_axis=0, tiled=True)
    results = results.reshape(experts * capacity, width)
    mixed = jnp.dot(
        weighting.T,
        results.astype(jnp.float32),
        precision=lax.Precision.HIGHEST,
        preferred_element_type=jnp.float32,
    )
    return mixed.astype(jnp.bfloat16)


def norm_body(experts, tok_hbm, ids_hbm, score_hbm, gain_hbm, *refs):
    outs, (tok_ref, ids_ref, score_ref, gain_ref, sems) = refs[:-5], refs[-5:]
    pairs = [(ids_hbm, ids_ref), (score_hbm, score_ref), (tok_hbm, tok_ref), (gain_hbm, gain_ref)]
    copies = [pltpu.make_async_copy(src, dst, sems.at[i]) for i, (src, dst) in enumerate(pairs)]
    for copy in copies:
        copy.start()
    rows, width = tok_ref.shape
    copies[0].wait()
    copies[1].wait()
    lane = lax.broadcasted_iota(jnp.int32, (rows, LANES), 1)
    expert = lax.rem(lane, experts).astype(jnp.float32)
    square = (rows, rows)
    diagonal = lax.broadcasted_iota(jnp.int32, square, 0) == lax.broadcasted_iota(jnp.int32, square, 1)

    def column(row):
        return jnp.sum(jnp.where(diagonal, jnp.broadcast_to(row, square), 0.0), axis=1, keepdims=True)

    weight = jnp.zeros((rows, LANES), jnp.float32)
    for k in range(ids_ref.shape[0]):
        chosen = column(ids_ref[k:k + 1, :].astype(jnp.float32))
        weight += jnp.where(chosen == expert, column(score_ref[k:k + 1, :]), 0.0)
    high = weight.astype(jnp.bfloat16).astype(jnp.float32)
    rest = weight - high
    middle = rest.astype(jnp.bfloat16).astype(jnp.float32)
    low = rest - middle
    term = jnp.where(lane < experts, high, jnp.where(lane < 2 * experts, middle, low))
    term = jnp.where(lane < 3 * experts, term, 0.0).astype(jnp.bfloat16)
    part = rows // len(outs)
    for i, out_ref in enumerate(outs):
        out_ref[:, width:] = term[i * part:(i + 1) * part]
    copies[2].wait()
    values = tok_ref[...].astype(jnp.float32)
    scale = lax.rsqrt(jnp.mean(values * values, axis=-1, keepdims=True) + 1e-05)
    copies[3].wait()
    normed = (values * scale * gain_ref[...]).astype(jnp.bfloat16)
    for i, out_ref in enumerate(outs):
        out_ref[:, :width] = normed[i * part:(i + 1) * part]


def norm_call(tokens, expert_ids, gate_scores, norm_gain, experts):
    rows, width = tokens.shape
    operands = (tokens, expert_ids.T, gate_scores.T, norm_gain.reshape(1, width))
    operands = [pltpu.with_memory_space_constraint(o, pltpu.HBM) for o in operands]
    return pl.pallas_call(
        functools.partial(norm_body, experts),
        out_shape=[jax.ShapeDtypeStruct((rows // PARTS, width + LANES), jnp.bfloat16)] * PARTS,
        in_specs=[pl.BlockSpec(memory_space=pltpu.HBM)] * 4,
        out_specs=[pl.BlockSpec(memory_space=pltpu.VMEM)] * PARTS,
        scratch_shapes=[pltpu.VMEM(o.shape, o.dtype) for o in operands] + [pltpu.SemaphoreType.DMA((4,))],
        compiler_params=pltpu.CompilerParams(vmem_limit_bytes=4 << 20),
    )(*operands)


def load_body(*refs):
    count = (len(refs) - 1) // 2
    copies = [pltpu.make_async_copy(refs[i], refs[count + i], refs[-1].at[i]) for i in range(count)]
    for copy in copies:
        copy.start()
    for copy in copies:
        copy.wait()


def load_call(*arrays):
    vmem = pl.BlockSpec(memory_space=pltpu.VMEM)
    return pl.pallas_call(
        load_body,
        out_shape=[jax.ShapeDtypeStruct(a.shape, a.dtype) for a in arrays],
        in_specs=[pl.BlockSpec(memory_space=pltpu.HBM)] * len(arrays),
        out_specs=[vmem] * len(arrays),
        scratch_shapes=[pltpu.SemaphoreType.DMA((len(arrays),))],
        compiler_params=pltpu.CompilerParams(vmem_limit_bytes=12 << 20),
    )(*[pltpu.with_memory_space_constraint(a, pltpu.HBM) for a in arrays])


def pack_body(*refs):
    part = refs[0].shape[0]
    for i, ref in enumerate(refs[:-1]):
        refs[-1][i * part:(i + 1) * part, :] = ref[...]


def pack_call(arrays):
    rows, width = arrays[0].shape
    vmem = pl.BlockSpec(memory_space=pltpu.VMEM)
    return pl.pallas_call(
        pack_body,
        out_shape=jax.ShapeDtypeStruct((len(arrays) * rows, width), arrays[0].dtype),
        in_specs=[vmem] * len(arrays),
        out_specs=vmem,
        compiler_params=pltpu.CompilerParams(vmem_limit_bytes=4 << 20),
    )(*arrays)


def added(terms):
    part = min(ref.shape[0] for ref, _ in terms)
    value = None
    for ref, row in terms:
        term = ref[row:row + part, :].astype(jnp.float32)
        value = term if value is None else value + term
    return value.astype(jnp.bfloat16)


def total_body(plan, *refs):
    for out, terms in zip(refs[-len(plan):], plan):
        out[...] = added([(refs[which], row) for which, row in terms])


def total_call(arrays, plan):
    shape = jax.ShapeDtypeStruct(min((a.shape for a in arrays), key=lambda s: s[0]), jnp.bfloat16)
    vmem = pl.BlockSpec(memory_space=pltpu.VMEM)
    return pl.pallas_call(
        functools.partial(total_body, plan),
        out_shape=[shape] * len(plan),
        in_specs=[vmem] * len(arrays),
        out_specs=[vmem] * len(plan),
        compiler_params=pltpu.CompilerParams(vmem_limit_bytes=4 << 20),
    )(*arrays)


def out_body(row, count, *refs):
    sum_ref, sem = refs[-2:]
    sum_ref[...] = added([(ref, 0) for ref in refs[:count]])
    copy = pltpu.make_async_copy(sum_ref, refs[-3].at[pl.ds(row, sum_ref.shape[0])], sem)
    copy.start()
    copy.wait()


def out_call(arrays, row, rows, held):
    part, width = arrays[0].shape
    vmem, hbm = pl.BlockSpec(memory_space=pltpu.VMEM), pl.BlockSpec(memory_space=pl.ANY)
    return pl.pallas_call(
        functools.partial(out_body, row, len(arrays)),
        out_shape=jax.ShapeDtypeStruct((rows, width), jnp.bfloat16),
        in_specs=[vmem] * len(arrays) + [hbm] * len(held),
        out_specs=hbm,
        scratch_shapes=[pltpu.VMEM((part, width), jnp.bfloat16), pltpu.SemaphoreType.DMA(())],
        input_output_aliases={len(arrays): 0} if held else {},
        compiler_params=pltpu.CompilerParams(vmem_limit_bytes=4 << 20),
    )(*arrays, *held)


def expert_call(blocks, weights, experts, rows):
    width = weights[2].shape[1]
    part = jax.ShapeDtypeStruct((rows // PARTS, width), jnp.bfloat16)
    vmem = pl.BlockSpec(memory_space=pltpu.VMEM)
    return pl.pallas_call(
        functools.partial(expert_body, experts),
        out_shape=[part] * (2 * PARTS) + [jax.ShapeDtypeStruct((rows, width), jnp.bfloat16)] * 2,
        in_specs=[vmem] * (len(blocks) + 3),
        out_specs=[vmem] * (2 * PARTS + 2),
        compiler_params=pltpu.CompilerParams(vmem_limit_bytes=20 << 20),
        cost_estimate=pl.CostEstimate(
            flops=24 * rows * width * weights[0].shape[1], bytes_accessed=16 << 20, transcendentals=0),
    )(*blocks, *weights)


def expert_body(experts, *refs):
    blocks, (gate_ref, up_ref, down_ref), outs = refs[:4], refs[4:7], refs[7:]
    width = down_ref.shape[1]
    pieces = [pl.ds(k, STEP) for k in range(0, width, STEP)]

    gate = up = None
    for piece in pieces:
        part = jnp.concatenate([b[:, piece] for b in blocks], axis=0)
        g = jnp.dot(part, gate_ref[piece, :], preferred_element_type=jnp.float32)
        u = jnp.dot(part, up_ref[piece, :], preferred_element_type=jnp.float32)
        gate = g if gate is None else gate + g
        up = u if up is None else up + u
    terms = jnp.concatenate([b[:, width:] for b in blocks], axis=0).astype(jnp.float32)
    lane = lax.broadcasted_iota(jnp.int32, terms.shape, 1)
    weight = jnp.sum(jnp.where(lax.rem(lane, experts) == lax.axis_index("expert"), terms, 0.0), axis=1, keepdims=True)
    hidden = gate / (1.0 + jnp.exp(-gate)) * up * weight
    hidden = jnp.where(weight == 0.0, 0.0, hidden).astype(jnp.bfloat16)
    for piece in pieces:
        part = jnp.dot(hidden, down_ref[:, piece], preferred_element_type=jnp.float32).astype(jnp.bfloat16)
        row = 0
        for out in outs:
            out[:, piece] = part[row:row + out.shape[0]]
            row += out.shape[0]


def gathered(tokens, expert_ids, gate_scores, norm_gain, w_gate, w_up, w_down):
    rows = tokens.shape[0]
    experts, slices = lax.axis_size("expert"), lax.axis_size("tensor")

    def swap(arrays, bit):
        return send(arrays, "tensor", [(i, i ^ bit) for i in range(slices)])

    ring = list(range(0, experts, 2)) + list(range(1, experts, 2))[::-1]

    def turn(arrays):
        return send(arrays, "expert", [(ring[i - 1], ring[i]) for i in range(experts)])

    def send(arrays, axis, pairs):
        out = []
        for array in arrays:
            out.append(lax.ppermute(array, axis, pairs))
        return out

    own = list(norm_call(tokens, expert_ids, gate_scores, norm_gain, experts))
    weights = load_call(w_gate[0], w_up[0], w_down[0])
    near = [own]
    for _ in range(1, experts):
        near.append(turn(near[-1]))
    far = [swap(near[s], 2) for s in range(experts - 1)]
    far.append(turn(far[-1]))
    part = rows // PARTS

    def packed(arrays):
        here = pack_call(arrays)
        return [here] + swap([here], 1)

    def both(mine, sibling):
        terms = mine + swap([sibling], 1)
        return total_call(terms, [[(i, 0), (PARTS, i * part)] for i in range(PARTS)])

    sums = []
    for s in range(experts):
        here, there = zip(packed(far[s]), packed(near[s]))
        *mine, other, sibling = expert_call([*here, *there], weights, experts, rows)
        swapped = swap(both(mine[:PARTS], other), 2)
        sums.append(list(zip(both(mine[PARTS:], sibling), swapped)))
    passed = [[] for _ in range(PARTS)]
    for s in range(1, experts):
        total = []
        for i in range(PARTS):
            terms = [*passed[i], *sums[s][i]]
            total += total_call(terms, [[(t, 0) for t in range(len(terms))]])
        passed = [[t] for t in turn(total)]
    result = []
    for i in range(PARTS):
        result = [out_call([*passed[i], *sums[0][i]], i * part, rows, result)]
    return result[0]


def is_dense(mesh_shape, rows):
    experts, slices = mesh_shape["expert"], mesh_shape["tensor"]
    return 4 * rows // experts >= rows and slices == 4 and experts > 2 and 3 * experts <= LANES


def on_device(tokens, *rest):
    shape = {name: lax.axis_size(name) for name in ("expert", "tensor")}
    plan = gathered if is_dense(shape, tokens.shape[0]) else routed
    return plan(tokens, *rest)


def solution(mesh):
    return jax.shard_map(
        on_device,
        mesh=mesh,
        in_specs=(
            P(("groups", "expert", "tensor"), None),
            P(("groups", "expert", "tensor"), None),
            P(("groups", "expert", "tensor"), None),
            P(),
            P("expert", None, "tensor"),
            P("expert", None, "tensor"),
            P("expert", "tensor", None),
        ),
        out_specs=P(("groups", "expert", "tensor"), None),
        check_vma=False,
    )
```
